32 devices in a mesh: ctx: 8 (over y, x, core), head: 4 (over z).
Axes of the slice: x: 2, y: 2, z: 4, core: 2. Of those that a mesh axis runs over, the one named last changes fastest.
Arguments:
- query_key: bfloat16 [4096, 1024], P('ctx', 'head'), may hold values from -6 to 6
- values: bfloat16 [4096, 4096], P('ctx', 'head'), may hold values from -6 to 6
- out_grad: bfloat16 [4096, 4096], P('ctx', 'head'), may hold values from -6 to 6
- out_weight: bfloat16 [4096, 4096], P('head'), may hold values from -0.09375 to 0.09375
- doc_lengths: int32 [32], replicated, may hold values from 1 to 2048, 4096 in all
Outputs:
- qk_grad: bfloat16 [4096, 1024], P('ctx', 'head')
- value_grad: bfloat16 [4096, 4096], P('ctx', 'head')
- proj_grad: float32 [4096, 4096], P('head', 'ctx')
The draws below stay inside these ranges and needn't reach their ends.
Inputs may be any that keep to these rules, and one draw needn't show every extreme that they name: `doc_lengths`: the documents fill all 4096 positions in order; the longest has exactly 2048 tokens.
All inputs are finite; a program needn't handle non-finite values.
Results may differ from the reference program's by a relative error of at most 0.0068.
Values may be sent and summed in bfloat16 or wider, within the bound.
A program may use at most 128 MiB of HBM per device.

```python
import math
import jax
import jax.numpy as jnp
import numpy as np
from jax import lax

D = 4096
H = 32
HEAD = 128
QK = 16
FEAT = 273
T_DEV = 512
NTOK = 4096
NDOC = 32
DOC_MOST = 2048
N_CTX = 8


def raised(values, own_key, source, target, blocks, factor):
    owner, partner = [(jnp.arange(values.shape[axis_at]) // (values.shape[axis_at] // blocks)).reshape([-1 if axis == axis_at else 1 for axis in range(values.ndim)]) for axis_at in (source, target)]
    chosen = jax.random.permutation(own_key, blocks)[partner]
    strong = (owner == chosen) | (owner == (partner + blocks // 2) % blocks)
    return jnp.where(strong, factor * values, values)


def block_scale(rng, dims, cuts, smallest, high):
    def one(dim, parts):
        steps = jax.random.uniform(jax.random.fold_in(jax.random.fold_in(rng, 6), dim), (parts,), jnp.float32, smallest / len(cuts), high / len(cuts))
        return jnp.repeat(jnp.exp(steps), dims[dim] // parts).reshape((-1,) + (1,) * (len(dims) - dim - 1))

    factor_of = one(*cuts[0])
    for cut in cuts[1:]:
        factor_of = factor_of * one(*cut)
    return factor_of


def profile(count, total, reach, skew):
    portions = [(1 << 20) // math.isqrt(grade ** skew) + 1 for grade in range(2, count + 1)]
    surplus, holding = total - reach - (count - 1), [1] * (count - 1)
    while surplus > 0:
        movable = [i for i in range(count - 1) if holding[i] < reach]
        mass, left = sum([portions[i] for i in movable]), surplus
        for i in movable:
            more = min(reach - holding[i], max(1, left * portions[i] // mass), surplus)
            holding[i] = holding[i] + more
            surplus = surplus - more
    return np.array([reach] + holding)


def ragged_sizes(own_key, amount, total, bound, slope):
    if amount == 2:
        one = jax.random.randint(own_key, (), max(1, total - bound), min(bound, total - 1) + 1)
        return jnp.stack([one, total - one])
    lengths = jnp.asarray(profile(amount, total, bound, slope), jnp.int32)
    pairs = (amount - 1) // 2
    source_of, taker = lengths[1:1 + 2 * pairs:2], lengths[2:2 + 2 * pairs:2]
    slack = jnp.minimum(source_of - 1, bound - taker)
    passed = jax.random.randint(jax.random.fold_in(own_key, 1), (pairs,), 0, 1 << 20) % (slack + 1)
    lengths = lengths.at[1:1 + 2 * pairs:2].set(source_of - passed).at[2:2 + 2 * pairs:2].set(taker + passed)
    return lengths[jax.random.permutation(jax.random.fold_in(own_key, 2), amount)]


def noise(key, dims, width, reach, pieces=(), kind=jnp.bfloat16):
    values = jax.random.normal(key, dims, jnp.float32) * width
    if len(pieces) > 0:
        values = block_scale(key, dims, pieces, -0.22, 0.18) * values
    return jnp.clip(values, min=-reach, max=reach).astype(kind)


def gaussian_with(stream_key, extent, deviation, limit, shards, heavy, held_as=jnp.bfloat16):
    entries = deviation * jax.random.normal(stream_key, extent, jnp.float32)
    if shards:
        entries = entries * block_scale(stream_key, extent, shards, -0.22, 0.18)
    return jnp.clip(raised(entries, jax.random.fold_in(stream_key, 3), *heavy), -limit, limit).astype(held_as)


def setup_inputs(seed: int = 0) -> dict:
    seeds = jax.random.split(jax.random.key(seed), 6)
    return {
        "query_key": noise(seeds[0], (NTOK, H * 2 * QK), 1.0, 6.0, ((0, 8), (1, 4))),
        "values": noise(seeds[1], (NTOK, H * HEAD), 1.0, 6.0, ((0, 8), (1, 4))),
        "out_grad": gaussian_with(seeds[2], (NTOK, D), 1.0, 6.0, ((0, 8), (1, 4)), (0, 1, 8, 2.0)),
        "out_weight": noise(seeds[3], (H * HEAD, D), (H * HEAD) ** -0.5, 0.09375, ((0, 4),)),
        "doc_lengths": ragged_sizes(seeds[4], NDOC, NTOK, DOC_MOST, 2).astype(jnp.int32),
    }


quad_scale = 0.25 / math.sqrt(2.0)
highest = lax.Precision.HIGHEST

def rounded(array):
    return lax.optimization_barrier(array.astype(jnp.bfloat16)).astype(jnp.float32)

def features(points):
    feat_width = points.shape[-1]
    constant = jnp.ones(points.shape[:-1] + (1,), jnp.float32)
    products = (points[..., :, None] * points[..., None, :]).reshape(points.shape[:-1] + (feat_width * feat_width,))
    return jnp.concatenate([constant, points * 0.5, products * quad_scale], axis=-1)

def feature_grad(grad_feat, points):
    feat_width = points.shape[-1]
    linear = grad_feat[..., 1:1 + feat_width] * 0.5
    square = grad_feat[..., 1 + feat_width:].reshape(points.shape[:-1] + (feat_width, feat_width))
    paired = square + jnp.swapaxes(square, -1, -2)
    return linear + quad_scale * lax.optimization_barrier(jnp.sum(paired * points[..., None, :], axis=-1))

def segment_ids(doc_lengths, positions):
    starts = (jnp.cumsum(doc_lengths, dtype=jnp.int32) - doc_lengths).astype(jnp.int32)
    return lax.optimization_barrier(jnp.sum((starts[None, :] <= positions[:, None]).astype(jnp.int32), axis=1)).astype(jnp.int32) - 1

def reference(query_key, values, out_grad, out_weight, doc_lengths):
    positions = jnp.arange(NTOK, dtype=jnp.int32)
    segment = segment_ids(doc_lengths, positions).reshape(N_CTX, T_DEV)
    previous = segment_ids(doc_lengths, positions - 1).reshape(N_CTX, T_DEV)
    open_before = previous[:, 0]
    open_after = segment[:, T_DEV - 1]
    restart = (open_after != open_before).astype(jnp.float32)
    carried = (segment == open_before[:, None]).astype(jnp.float32)
    ending = (segment == open_after[:, None]).astype(jnp.float32)
    paired = query_key.reshape(N_CTX, T_DEV, H, 2, QK).transpose(0, 2, 3, 1, 4)
    value_rows = values.reshape(N_CTX, T_DEV, H, HEAD).transpose(0, 2, 1, 3)
    upstream_all = jnp.dot(out_grad, out_weight.T, preferred_element_type=jnp.float32)
    upstream_all = upstream_all.reshape(N_CTX, T_DEV, H, HEAD).transpose(0, 2, 1, 3)

    def local_state(items):
        keys_part, value_part, ending_part = items
        key_feat = rounded(features(keys_part.astype(jnp.float32)))
        masked = key_feat * ending_part[None, :, None]
        state_part = jnp.einsum('htf,htd->hfd', masked, value_part.astype(jnp.float32), precision=highest)
        return (state_part, lax.optimization_barrier(jnp.sum(masked, axis=1)))
    state_local, norm_local = lax.map(local_state, (paired[:, :, 1], value_rows, ending))

    def forward_step(carry, items):
        state_part, norm_part, restart_part = items
        retained = 1.0 - restart_part
        return ((state_part + retained * carry[0], norm_part + retained * carry[1]), carry)
    zeros_state = (jnp.zeros((H, FEAT, HEAD), jnp.float32), jnp.zeros((H, FEAT), jnp.float32))
    unused, (state_in, norm_in) = lax.scan(forward_step, zeros_state, (state_local, norm_local, restart))

    def local_grads(items):
        queries, keys_all, value_part, upstream, segment_part, near_rows, state_part, norm_part = items
        places = jnp.arange(T_DEV, dtype=jnp.int32)
        query_float = queries.astype(jnp.float32)
        key_float = keys_all.astype(jnp.float32)
        value_float = value_part.astype(jnp.float32)
        query_feat = rounded(features(query_float))
        state_r = rounded(state_part)
        scores = jnp.einsum('hid,hjd->hij', query_float, key_float, precision=highest) * 0.25
        visible = (places[None, :] <= places[:, None]) & (segment_part[:, None] == segment_part[None, :])
        weight = jnp.where(visible[None], 1.0 + scores + 0.5 * scores * scores, 0.0)
        weight_r = rounded(weight)
        from_state = jnp.einsum('hif,hfd->hid', query_feat, state_r, precision=highest)
        numerator = jnp.einsum('hij,hjd->hid', weight_r, value_float, precision=highest) + near_rows[None, :, None] * from_state
        denominator = lax.optimization_barrier(jnp.sum(weight, axis=2)) + near_rows[None, :] * jnp.einsum('hif,hf->hi', query_feat, norm_part, precision=highest)
        attended = numerator / denominator[:, :, None]
        den_grad = -lax.optimization_barrier(jnp.sum(upstream * attended, axis=2)) / denominator
        num_float = rounded(upstream / denominator[:, :, None])
        mix_grad = jnp.einsum('hid,hjd->hij', num_float, value_float, precision=highest) + den_grad[:, :, None]
        score_grad = rounded(jnp.where(visible[None], mix_grad * (1.0 + scores), 0.0))
        value_grad = jnp.einsum('hij,hid->hjd', weight_r, num_float, precision=highest)
        key_grad = 0.25 * jnp.einsum('hij,hid->hjd', score_grad, query_float, precision=highest)
        feat_grad = near_rows[None, :, None] * (jnp.einsum('hid,hfd->hif', num_float, state_r, precision=highest) + den_grad[:, :, None] * norm_part[:, None, :])
        query_grad = 0.25 * jnp.einsum('hij,hjd->hid', score_grad, key_float, precision=highest) + feature_grad(feat_grad, query_float)
        near_feat = query_feat * near_rows[None, :, None]
        adj_part = jnp.einsum('hif,hid->hfd', near_feat, num_float, precision=highest)
        nadj_part = jnp.einsum('hif,hi->hf', near_feat, den_grad, precision=highest)
        return (attended.astype(jnp.bfloat16), query_grad.astype(jnp.bfloat16), key_grad, value_grad, adj_part, nadj_part)
    attended, query_grad, key_grad, value_grad, adj_local, nadj_local = lax.map(local_grads, (paired[:, :, 0], paired[:, :, 1], value_rows, upstream_all, segment, carried, state_in, norm_in))

    def backward_step(carry, items):
        adj_part, nadj_part, restart_part = items
        retained = 1.0 - restart_part
        return ((adj_part + retained * carry[0], nadj_part + retained * carry[1]), carry)
    unused, (adj_in, nadj_in) = lax.scan(backward_step, zeros_state, (adj_local, nadj_local, restart), reverse=True)

    def finish(items):
        keys_all, value_part, ending_part, key_part, value_part_grad, adj_part, nadj_part = items
        key_float = keys_all.astype(jnp.float32)
        key_feat = rounded(features(key_float))
        adj_r = rounded(adj_part)
        ending_col = ending_part[None, :, None]
        value_total = value_part_grad + ending_col * jnp.einsum('htf,hfd->htd', key_feat, adj_r, precision=highest)
        key_feat_grad = ending_col * (jnp.einsum('htd,hfd->htf', value_part.astype(jnp.float32), adj_r, precision=highest) + nadj_part[:, None, :])
        key_total = key_part + feature_grad(key_feat_grad, key_float)
        return (key_total.astype(jnp.bfloat16), value_total.astype(jnp.bfloat16))
    key_out, value_out = lax.map(finish, (paired[:, :, 1], value_rows, ending, key_grad, value_grad, adj_in, nadj_in))
    attended_flat = attended.transpose(0, 2, 1, 3).reshape(NTOK, H * HEAD)
    proj_grad = jnp.dot(attended_flat.T, out_grad, preferred_element_type=jnp.float32)
    qk_grad = jnp.stack([query_grad, key_out], axis=2).transpose(0, 3, 1, 2, 4).reshape(NTOK, H * 2 * QK)
    value_grad_out = value_out.transpose(0, 2, 1, 3).reshape(NTOK, H * HEAD)
    return (qk_grad, value_grad_out, proj_grad)
```

```python
import math

import jax
import jax.numpy as jnp
import numpy as np
from jax import lax
from jax.sharding import PartitionSpec as P

HEAD = 128
QK = 16
CHIP_SPAN = 2

quad_scale = 0.25 / math.sqrt(2.0)

bf16 = jnp.bfloat16
f32 = jnp.float32

PAIRS = [(a, b) for a in range(QK) for b in range(a, QK)]
KEPT = 1 + QK + len(PAIRS)
FEAT = 160


def tables():
    left = np.zeros((QK, FEAT), np.float32)
    right = np.zeros((QK, FEAT), np.float32)
    left_add = np.zeros((FEAT,), np.float32)
    right_add = np.zeros((FEAT,), np.float32)
    scale = np.zeros((FEAT,), np.float32)
    weight = np.ones((FEAT,), np.float32)
    left_add[0] = right_add[0] = scale[0] = 1.0
    for a in range(QK):
        left[a, 1 + a] = 1.0
        right_add[1 + a] = 1.0
        scale[1 + a] = 0.5
    for place, (a, b) in enumerate(PAIRS):
        left[a, 1 + QK + place] = 1.0
        right[b, 1 + QK + place] = 1.0
        scale[1 + QK + place] = quad_scale
        weight[1 + QK + place] = 1.0 if a == b else 2.0
    return left, right, left_add, right_add, scale, weight


LEFT, RIGHT, LEFT_ADD, RIGHT_ADD, SCALE, WEIGHT = tables()


def dot(spec, a, b):
    return jnp.einsum(spec, a, b, preferred_element_type=f32)


def factors(points):
    first = dot("htd,df->htf", points, jnp.asarray(LEFT, bf16)) + LEFT_ADD
    second = dot("htd,df->htf", points, jnp.asarray(RIGHT, bf16)) + RIGHT_ADD
    return first, second


def feature_grad(grad_feat, first, second):
    scaled = grad_feat * (SCALE * WEIGHT)
    return dot("htf,df->htd", (scaled * second).astype(bf16), jnp.asarray(LEFT, bf16)) + dot(
        "htf,df->htd", (scaled * first).astype(bf16), jnp.asarray(RIGHT, bf16)
    )


def segment_ids(doc_lengths, positions):
    starts = jnp.cumsum(doc_lengths, dtype=jnp.int32) - doc_lengths
    return jnp.sum((starts[None, :] <= positions[:, None]).astype(jnp.int32), axis=1) - 1


def chip_shift(parts, chips, steps):
    moves = [
        (2 * c + core, 2 * (c + steps) + core)
        for c in range(chips)
        for core in range(2)
        if 0 <= c + steps < chips
    ]
    return [lax.ppermute(part, "ctx", moves) for part in parts]


def swap(parts, count):
    return [lax.ppermute(part, "ctx", [(c, c ^ 1) for c in range(count)]) for part in parts]


def carried_in(parts, edges, step, count):
    index = lax.axis_index("ctx")
    core = index % 2
    sent = [parts[0].astype(bf16), parts[1]]
    other = swap(sent, count)
    early = core == (0 if step > 0 else 1)
    near = [jnp.where(early, o, s).astype(f32) for o, s in zip(other, sent)]
    far = [jnp.where(early, s, o).astype(f32) for o, s in zip(other, sent)]
    chip = index // 2

    def keep(block):
        inside = (block >= 0) & (block < count)
        return jnp.where(inside & (edges(block) == edges(block + 1)), 1.0, 0.0)

    near_block = 2 * chip + (1 if step > 0 else 0)
    keep_near = keep(near_block)
    pair = [(n + keep_near * f).astype(s.dtype) for n, f, s in zip(near, far, sent)]
    arrived = [chip_shift(pair, count // 2, step * (k + 1)) for k in range(CHIP_SPAN)]
    total = [a.astype(f32) for a in arrived[0]]
    through = jnp.float32(1.0)
    for k in range(1, CHIP_SPAN):
        base = 2 * (chip - step * k)
        through = through * keep(base) * keep(base + 1)
        total = [t + through * a.astype(f32) for t, a in zip(total, arrived[k])]
    first_kept = keep(2 * chip + (0 if step > 0 else 1))
    late = [f + first_kept * t for f, t in zip(far, total)]
    return [jnp.where(early, t, l) for t, l in zip(total, late)]


def reduce_halves(attended, full_out, count):
    index = lax.axis_index("ctx")
    chip, core = index // 2, index % 2
    chips = count // 2
    width = full_out.shape[1] // count
    rows = attended.shape[1]

    def columns(parity):
        return [
            lax.dynamic_slice_in_dim(full_out, (((r ^ chip) * 2) + parity) * width, width, 1)
            for r in range(chips)
        ]

    def product(picked):
        return lax.dot_general(
            attended,
            jnp.concatenate(picked, axis=1),
            (((0,), (0,)), ((), ())),
            preferred_element_type=f32,
        )

    leaving = product(columns(1 - core)).astype(bf16)
    (came,) = swap([leaving], count)
    mine = product(columns(core)) + came.astype(f32)
    bits = max(1, chips).bit_length() - 1
    half = rows // 2
    flows = []
    for flow, order in ((0, list(range(bits))), (1, list(range(bits))[::-1])):
        held = {
            r: mine[flow * half : (flow + 1) * half, r * width : (r + 1) * width]
            for r in range(chips)
        }
        for bit in order:
            moving = [r for r in held if (r >> bit) & 1]
            packed = jnp.concatenate([held[r].astype(bf16) for r in moving], axis=1)
            got = lax.ppermute(
                packed,
                "ctx",
                [(2 * c + k, 2 * (c ^ (1 << bit)) + k) for c in range(chips) for k in range(2)],
            )
            for place, r in enumerate(moving):
                target = r ^ (1 << bit)
                held[target] = held[target] + got[:, place * width : (place + 1) * width].astype(f32)
                del held[r]
        flows.append(held[0])
    return jnp.concatenate(flows, axis=0)


def on_device(query_key, values, out_grad, out_weight, doc_lengths):
    tokens = query_key.shape[0]
    head_count = out_weight.shape[0] // HEAD
    count = lax.axis_size("ctx")
    depth = lax.axis_size("head")
    level = lax.axis_index("head")
    shard = out_grad.shape[1]
    index = lax.axis_index("ctx")
    offset = index * tokens

    upward, downward, pieces = out_grad, out_grad, [(out_grad, level)]
    for k in range(1, depth):
        upward = lax.ppermute(upward, "head", [(i, i + 1) for i in range(k - 1, depth - 1)])
        downward = lax.ppermute(downward, "head", [(i, i - 1) for i in range(1, depth - k + 1)])
        if 2 * k >= depth:
            pieces.append(
                (
                    jnp.where(level >= k, upward, downward),
                    jnp.where(level >= k, level - k, jnp.minimum(level + k, depth - 1)),
                    (level >= k) | (level + k < depth),
                )
            )
        else:
            pieces.append((upward, jnp.maximum(level - k, 0), level >= k))
            pieces.append((downward, jnp.minimum(level + k, depth - 1), level + k < depth))
    out_rows = jnp.zeros((tokens, out_weight.shape[0]), f32)
    full_out = jnp.zeros((tokens, shard * depth), bf16)
    for piece in pieces:
        part, owner = piece[0], piece[1]
        weight_part = lax.dynamic_slice_in_dim(out_weight, owner * shard, shard, 1)
        out_rows = out_rows + lax.dot_general(
            part, weight_part, (((1,), (1,)), ((), ())), preferred_element_type=f32
        )
        if len(piece) == 3:
            old = lax.dynamic_slice_in_dim(full_out, owner * shard, shard, 1)
            part = jnp.where(piece[2], part, old)
        full_out = lax.dynamic_update_slice_in_dim(full_out, part, owner * shard, 1)

    starts = jnp.cumsum(doc_lengths, dtype=jnp.int32) - doc_lengths

    def edges(block):
        return jnp.sum((starts <= block * tokens - 1).astype(jnp.int32)) - 1

    positions = offset + jnp.arange(tokens, dtype=jnp.int32)
    segment = segment_ids(doc_lengths, positions)
    open_before = edges(index)
    open_after = segment[tokens - 1]
    carried = (segment == open_before).astype(f32)[None, :, None]
    ending = (segment == open_after).astype(f32)[None, :, None]
    paired = query_key.reshape(tokens, head_count, 2, QK).transpose(1, 2, 0, 3)
    queries = paired[:, 0]
    keys_all = paired[:, 1]
    value_rows = values.reshape(tokens, head_count, HEAD).transpose(1, 0, 2)
    query_first, query_second = factors(queries)
    key_first, key_second = factors(keys_all)
    query_feat = (query_first * query_second * SCALE).astype(bf16)
    key_feat = (key_first * key_second * SCALE).astype(bf16)
    ending_feat = jnp.where(ending > 0.5, key_feat, jnp.zeros_like(key_feat))
    state_local = dot("htf,htd->hfd", ending_feat, value_rows)
    norm_local = jnp.sum(ending_feat.astype(f32), axis=1)
    state_in, norm_in = carried_in([state_local, norm_local], edges, 1, count)
    state_b = state_in.astype(bf16)
    query_weighted = query_feat * jnp.asarray(WEIGHT, bf16)
    places = jnp.arange(tokens, dtype=jnp.int32)
    scores = dot("hid,hjd->hij", queries, keys_all) * 0.25
    visible = (places[None, :] <= places[:, None]) & (segment[:, None] == segment[None, :])
    weight = jnp.where(visible[None], 1.0 + scores + 0.5 * scores * scores, 0.0)
    weight_b = weight.astype(bf16)
    from_state = dot("hif,hfd->hid", query_weighted, state_b)
    numerator = dot("hij,hjd->hid", weight_b, value_rows) + carried * from_state
    denominator = (
        jnp.sum(weight, axis=2, keepdims=True)
        + carried
        * jnp.sum(query_weighted.astype(f32) * norm_in[:, None, :], axis=2, keepdims=True)
    )
    attended = numerator / denominator
    attended_all = (
        attended.astype(bf16).transpose(1, 0, 2).reshape(tokens, head_count * HEAD)
    )
    proj_grad = reduce_halves(attended_all, full_out, count)

    grads_out = out_rows.reshape(tokens, head_count, HEAD).transpose(1, 0, 2)
    den_grad = -jnp.sum(grads_out * attended, axis=2, keepdims=True) / denominator
    num_grad = (grads_out / denominator).astype(bf16)
    near_feat = jnp.where(carried > 0.5, query_feat, jnp.zeros_like(query_feat))
    adj_local = dot("hif,hid->hfd", near_feat, num_grad)
    nadj_local = jnp.sum(near_feat.astype(f32) * den_grad, axis=1)
    adj_in, nadj_in = carried_in([adj_local, nadj_local], edges, -1, count)
    adjoint_b = adj_in.astype(bf16)

    mix_grad = dot("hid,hjd->hij", num_grad, value_rows) + den_grad
    score_grad = jnp.where(visible[None], mix_grad * (1.0 + scores), 0.0).astype(bf16)
    value_grad = dot("hij,hid->hjd", weight_b, num_grad)
    key_grad = 0.25 * dot("hij,hid->hjd", score_grad, queries)
    feat_grad = carried * (
        dot("hid,hfd->hif", num_grad, state_b) + den_grad * norm_in[:, None, :]
    )
    query_grad = 0.25 * dot("hij,hjd->hid", score_grad, keys_all) + feature_grad(
        feat_grad, query_first, query_second
    )
    value_grad = value_grad + ending * dot(
        "htf,hfd->htd", key_feat * jnp.asarray(WEIGHT, bf16), adjoint_b
    )
    key_feat_grad = ending * (
        dot("htd,hfd->htf", value_rows, adjoint_b) + nadj_in[:, None, :]
    )
    key_grad = key_grad + feature_grad(key_feat_grad, key_first, key_second)
    qk_grad = (
        jnp.stack([query_grad, key_grad], axis=2)
        .transpose(1, 0, 2, 3)
        .reshape(tokens, head_count * 2 * QK)
        .astype(bf16)
    )
    value_out = (
        value_grad.transpose(1, 0, 2).reshape(tokens, head_count * HEAD).astype(bf16)
    )
    return (qk_grad, value_out, proj_grad)


def solution(mesh):
    placed = (P("ctx", "head"), P("ctx", "head"), P("ctx", "head"), P("head", None), P())
    return jax.shard_map(
        on_device,
        mesh=mesh,
        in_specs=placed,
        out_specs=(P("ctx", "head"), P("ctx", "head"), P("head", "ctx")),
        check_vma=False,
    )
```

```python
import math

import jax
import jax.numpy as jnp
import numpy as np
from jax import lax
from jax.sharding import PartitionSpec as P

HEAD = 128
QK = 16
CHIP_SPAN = 2
CHUNK = 256

quad_scale = 0.25 / math.sqrt(2.0)

bf16 = jnp.bfloat16
f32 = jnp.float32

PAIRS = [(a, b) for a in range(QK) for b in range(a, QK)]
KEPT = 1 + QK + len(PAIRS)
FEAT = 160


def tables():
    left = np.zeros((QK, FEAT), np.float32)
    right = np.zeros((QK, FEAT), np.float32)
    left_add = np.zeros((FEAT,), np.float32)
    right_add = np.zeros((FEAT,), np.float32)
    scale = np.zeros((FEAT,), np.float32)
    weight = np.ones((FEAT,), np.float32)
    left_add[0] = right_add[0] = scale[0] = 1.0
    for a in range(QK):
        left[a, 1 + a] = 1.0
        right_add[1 + a] = 1.0
        scale[1 + a] = 0.5
    for place, (a, b) in enumerate(PAIRS):
        left[a, 1 + QK + place] = 1.0
        right[b, 1 + QK + place] = 1.0
        scale[1 + QK + place] = quad_scale
        weight[1 + QK + place] = 1.0 if a == b else 2.0
    return left, right, left_add, right_add, scale, weight


LEFT, RIGHT, LEFT_ADD, RIGHT_ADD, SCALE, WEIGHT = tables()


def dot(spec, a, b):
    return jnp.einsum(spec, a, b, preferred_element_type=f32)


def factors(points):
    first = dot("htd,df->htf", points, jnp.asarray(LEFT, bf16)) + LEFT_ADD
    second = dot("htd,df->htf", points, jnp.asarray(RIGHT, bf16)) + RIGHT_ADD
    return first, second


def feature_grad(grad_feat, first, second):
    scaled = grad_feat * (SCALE * WEIGHT)
    return dot("htf,df->htd", (scaled * second).astype(bf16), jnp.asarray(LEFT, bf16)) + dot(
        "htf,df->htd", (scaled * first).astype(bf16), jnp.asarray(RIGHT, bf16)
    )


def segment_ids(doc_lengths, positions):
    starts = jnp.cumsum(doc_lengths, dtype=jnp.int32) - doc_lengths
    return jnp.sum((starts[None, :] <= positions[:, None]).astype(jnp.int32), axis=1) - 1


def chip_shift(part, chips, steps):
    moves = [
        (2 * c + core, 2 * (c + steps) + core)
        for c in range(chips)
        for core in range(2)
        if 0 <= c + steps < chips
    ]
    return lax.ppermute(part, "ctx", moves)


def joined(state, norm):
    half = norm.shape[1] // 2
    high = norm.astype(bf16).astype(f32)
    low = norm - high
    rows = jnp.stack([high[:, :half], high[:, half:], low[:, :half], low[:, half:]], axis=1)
    rows = jnp.pad(rows, ((0, 0), (KEPT, FEAT - KEPT - 4), (0, HEAD - half)))
    return (state + rows).astype(bf16)


def parted(packed):
    half = FEAT // 2
    rows = packed[:, KEPT : KEPT + 4, :half].astype(f32)
    norm = jnp.concatenate([rows[:, 0] + rows[:, 2], rows[:, 1] + rows[:, 3]], axis=1)
    inside = (jnp.arange(FEAT) < KEPT)[None, :, None]
    return jnp.where(inside, packed.astype(f32), 0.0), norm


def carried_in(sent, edges, step, count):
    index = lax.axis_index("ctx")
    core = index % 2
    other = lax.ppermute(sent, "ctx", [(c, c ^ 1) for c in range(count)])
    early = core == (0 if step > 0 else 1)
    near = parted(jnp.where(early, other, sent))
    far = parted(jnp.where(early, sent, other))
    chip = index // 2

    def keep(block):
        inside = (block >= 0) & (block < count)
        return jnp.where(inside & (edges(block) == edges(block + 1)), 1.0, 0.0)

    keep_near = keep(2 * chip + (1 if step > 0 else 0))
    pair = joined(*[n + keep_near * f for n, f in zip(near, far)])
    arrived = [parted(chip_shift(pair, count // 2, step * (k + 1))) for k in range(CHIP_SPAN)]
    total = list(arrived[0])
    through = jnp.float32(1.0)
    for k in range(1, CHIP_SPAN):
        base = 2 * (chip - step * k)
        through = through * keep(base) * keep(base + 1)
        total = [t + through * a for t, a in zip(total, arrived[k])]
    first_kept = keep(2 * chip + (0 if step > 0 else 1))
    return [jnp.where(early, t, f + first_kept * t) for f, t in zip(far, total)]


def reduce_halves(attended, full_out, count):
    index = lax.axis_index("ctx")
    chip, core = index // 2, index % 2
    chips = count // 2
    width = full_out.shape[1] // count
    rows = attended.shape[1]

    def columns(parity):
        return [
            lax.dynamic_slice_in_dim(full_out, (((r ^ chip) * 2) + parity) * width, width, 1)
            for r in range(chips)
        ]

    def product(picked):
        return lax.dot_general(
            attended,
            jnp.concatenate(picked, axis=1),
            (((0,), (0,)), ((), ())),
            preferred_element_type=f32,
        )

    leaving = product(columns(1 - core)).astype(bf16)
    came = lax.ppermute(leaving, "ctx", [(c, c ^ 1) for c in range(count)])
    mine = product(columns(core)) + came.astype(f32)
    bits = max(1, chips).bit_length() - 1
    half = rows // 2
    flows = []
    for flow, order in ((0, list(range(bits))), (1, list(range(bits))[::-1])):
        held = {
            r: mine[flow * half : (flow + 1) * half, r * width : (r + 1) * width]
            for r in range(chips)
        }
        for bit in order:
            moving = [r for r in held if (r >> bit) & 1]
            packed = jnp.concatenate([held[r].astype(bf16) for r in moving], axis=1)
            got = lax.ppermute(
                packed,
                "ctx",
                [(2 * c + k, 2 * (c ^ (1 << bit)) + k) for c in range(chips) for k in range(2)],
            )
            for place, r in enumerate(moving):
                target = r ^ (1 << bit)
                held[target] = held[target] + got[:, place * width : (place + 1) * width].astype(f32)
                del held[r]
        flows.append(held[0])
    return jnp.concatenate(flows, axis=0)


def on_device(query_key, values, out_grad, out_weight, doc_lengths):
    tokens = query_key.shape[0]
    head_count = out_weight.shape[0] // HEAD
    count = lax.axis_size("ctx")
    depth = lax.axis_size("head")
    shard = out_grad.shape[1]
    index = lax.axis_index("ctx")
    offset = index * tokens

    owners = count // depth
    width = shard // owners
    chunks = max(1, width // CHUNK)
    sub = width // chunks
    cut = out_grad.reshape(tokens, owners, chunks, sub)
    cut_weight = out_weight.reshape(-1, count, chunks, sub)
    gathered, out_rows, proj_parts = [], 0.0, []
    for h in range(chunks):
        whole = lax.all_gather(
            cut[:, :, h].reshape(tokens, owners * sub), "head", axis=1, tiled=True
        )
        gathered.append(whole)

    starts = jnp.cumsum(doc_lengths, dtype=jnp.int32) - doc_lengths

    def edges(block):
        return jnp.sum((starts <= block * tokens - 1).astype(jnp.int32)) - 1

    positions = offset + jnp.arange(tokens, dtype=jnp.int32)
    segment = segment_ids(doc_lengths, positions)
    open_before = edges(index)
    open_after = segment[tokens - 1]
    carried = (segment == open_before).astype(f32)[None, :, None]
    ending = (segment == open_after).astype(f32)[None, :, None]
    paired = query_key.reshape(tokens, head_count, 2, QK).transpose(1, 2, 0, 3)
    queries = paired[:, 0]
    keys_all = paired[:, 1]
    value_rows = values.reshape(tokens, head_count, HEAD).transpose(1, 0, 2)
    query_first, query_second = factors(queries)
    key_first, key_second = factors(keys_all)
    query_feat = (query_first * query_second * SCALE).astype(bf16)
    key_feat = (key_first * key_second * SCALE).astype(bf16)
    ending_feat = jnp.where(ending > 0.5, key_feat, jnp.zeros_like(key_feat))
    state_local = dot("htf,htd->hfd", ending_feat, value_rows)
    norm_local = jnp.sum(ending_feat.astype(f32), axis=1)
    state_in, norm_in = carried_in(joined(state_local, norm_local), edges, 1, count)
    state_b = state_in.astype(bf16)
    query_weighted = query_feat * jnp.asarray(WEIGHT, bf16)
    places = jnp.arange(tokens, dtype=jnp.int32)
    scores = dot("hid,hjd->hij", queries, keys_all) * 0.25
    visible = (places[None, :] <= places[:, None]) & (segment[:, None] == segment[None, :])
    weight = jnp.where(visible[None], 1.0 + scores + 0.5 * scores * scores, 0.0)
    weight_b = weight.astype(bf16)
    from_state = dot("hif,hfd->hid", query_weighted, state_b)
    numerator = dot("hij,hjd->hid", weight_b, value_rows) + carried * from_state
    denominator = (
        jnp.sum(weight, axis=2, keepdims=True)
        + carried
        * jnp.sum(query_weighted.astype(f32) * norm_in[:, None, :], axis=2, keepdims=True)
    )
    attended = numerator / denominator
    attended_all = (
        attended.astype(bf16).transpose(1, 0, 2).reshape(tokens, head_count * HEAD)
    )
    for h, whole in enumerate(gathered):
        if h > 0:
            whole, proj_parts[-1] = lax.optimization_barrier((whole, proj_parts[-1]))
            gathered[h] = whole
        out_rows = out_rows + lax.dot_general(
            whole,
            cut_weight[:, :, h].reshape(-1, count * sub),
            (((1,), (1,)), ((), ())),
            preferred_element_type=f32,
        )
        if h < chunks - 1:
            proj_parts.append(reduce_halves(attended_all, whole, count))

    grads_out = out_rows.reshape(tokens, head_count, HEAD).transpose(1, 0, 2)
    den_grad = -jnp.sum(grads_out * attended, axis=2, keepdims=True) / denominator
    num_grad = (grads_out / denominator).astype(bf16)
    near_feat = jnp.where(carried > 0.5, query_feat, jnp.zeros_like(query_feat))
    adj_local = dot("hif,hid->hfd", near_feat, num_grad)
    nadj_local = jnp.sum(near_feat.astype(f32) * den_grad, axis=1)
    adj_sent, last = lax.optimization_barrier((joined(adj_local, nadj_local), gathered[-1]))
    adj_in, nadj_in = carried_in(adj_sent, edges, -1, count)
    proj_parts.append(reduce_halves(attended_all, last, count))
    proj_grad = jnp.concatenate(proj_parts, axis=1)
    adjoint_b = adj_in.astype(bf16)

    mix_grad = dot("hid,hjd->hij", num_grad, value_rows) + den_grad
    score_grad = jnp.where(visible[None], mix_grad * (1.0 + scores), 0.0).astype(bf16)
    value_grad = dot("hij,hid->hjd", weight_b, num_grad)
    key_grad = 0.25 * dot("hij,hid->hjd", score_grad, queries)
    feat_grad = carried * (
        dot("hid,hfd->hif", num_grad, state_b) + den_grad * norm_in[:, None, :]
    )
    query_grad = 0.25 * dot("hij,hjd->hid", score_grad, keys_all) + feature_grad(
        feat_grad, query_first, query_second
    )
    value_grad = value_grad + ending * dot(
        "htf,hfd->htd", key_feat * jnp.asarray(WEIGHT, bf16), adjoint_b
    )
    key_feat_grad = ending * (
        dot("htd,hfd->htf", value_rows, adjoint_b) + nadj_in[:, None, :]
    )
    key_grad = key_grad + feature_grad(key_feat_grad, key_first, key_second)
    qk_grad = (
        jnp.stack([query_grad, key_grad], axis=2)
        .transpose(1, 0, 2, 3)
        .reshape(tokens, head_count * 2 * QK)
        .astype(bf16)
    )
    value_out = (
        value_grad.transpose(1, 0, 2).reshape(tokens, head_count * HEAD).astype(bf16)
    )
    return (qk_grad, value_out, proj_grad)


def solution(mesh):
    placed = (P("ctx", "head"), P("ctx", "head"), P("ctx", "head"), P("head", None), P())
    return jax.shard_map(
        on_device,
        mesh=mesh,
        in_specs=placed,
        out_specs=(P("ctx", "head"), P("ctx", "head"), P("head", "ctx")),
        check_vma=False,
    )
```

```python
import math

import jax
import jax.numpy as jnp
import numpy as np
from jax import lax
from jax.sharding import PartitionSpec as P

HEAD = 128
QK = 16
CHIP_SPAN = 2

quad_scale = 0.25 / math.sqrt(2.0)

bf16 = jnp.bfloat16
f32 = jnp.float32

PAIRS = [(a, b) for a in range(QK) for b in range(a, QK)]
KEPT = 1 + QK + len(PAIRS)
FEAT = 160


def tables():
    left = np.zeros((QK, FEAT), np.float32)
    right = np.zeros((QK, FEAT), np.float32)
    left_add = np.zeros((FEAT,), np.float32)
    right_add = np.zeros((FEAT,), np.float32)
    scale = np.zeros((FEAT,), np.float32)
    weight = np.ones((FEAT,), np.float32)
    left_add[0] = right_add[0] = scale[0] = 1.0
    for a in range(QK):
        left[a, 1 + a] = 1.0
        right_add[1 + a] = 1.0
        scale[1 + a] = 0.5
    for place, (a, b) in enumerate(PAIRS):
        left[a, 1 + QK + place] = 1.0
        right[b, 1 + QK + place] = 1.0
        scale[1 + QK + place] = quad_scale
        weight[1 + QK + place] = 1.0 if a == b else 2.0
    return left, right, left_add, right_add, scale, weight


LEFT, RIGHT, LEFT_ADD, RIGHT_ADD, SCALE, WEIGHT = tables()


def dot(spec, a, b):
    return jnp.einsum(spec, a, b, preferred_element_type=f32)


def factors(points):
    first = dot("htd,df->htf", points, jnp.asarray(LEFT, bf16)) + LEFT_ADD
    second = dot("htd,df->htf", points, jnp.asarray(RIGHT, bf16)) + RIGHT_ADD
    return first, second


def feature_grad(grad_feat, first, second):
    scaled = grad_feat * (SCALE * WEIGHT)
    return dot("htf,df->htd", (scaled * second).astype(bf16), jnp.asarray(LEFT, bf16)) + dot(
        "htf,df->htd", (scaled * first).astype(bf16), jnp.asarray(RIGHT, bf16)
    )


def segment_ids(doc_lengths, positions):
    starts = jnp.cumsum(doc_lengths, dtype=jnp.int32) - doc_lengths
    return jnp.sum((starts[None, :] <= positions[:, None]).astype(jnp.int32), axis=1) - 1


def chip_shift(part, chips, steps):
    moves = [
        (2 * c + core, 2 * (c + steps) + core)
        for c in range(chips)
        for core in range(2)
        if 0 <= c + steps < chips
    ]
    return lax.ppermute(part, "ctx", moves)


def joined(state, norm):
    half = norm.shape[1] // 2
    high = norm.astype(bf16).astype(f32)
    low = norm - high
    rows = jnp.stack([high[:, :half], high[:, half:], low[:, :half], low[:, half:]], axis=1)
    rows = jnp.pad(rows, ((0, 0), (KEPT, FEAT - KEPT - 4), (0, HEAD - half)))
    return (state + rows).astype(bf16)


def parted(packed):
    half = FEAT // 2
    rows = packed[:, KEPT : KEPT + 4, :half].astype(f32)
    norm = jnp.concatenate([rows[:, 0] + rows[:, 2], rows[:, 1] + rows[:, 3]], axis=1)
    inside = (jnp.arange(FEAT) < KEPT)[None, :, None]
    return jnp.where(inside, packed.astype(f32), 0.0), norm


def carried_in(sent, edges, step, count):
    index = lax.axis_index("ctx")
    core = index % 2
    other = lax.ppermute(sent, "ctx", [(c, c ^ 1) for c in range(count)])
    early = core == (0 if step > 0 else 1)
    near = parted(jnp.where(early, other, sent))
    far = parted(jnp.where(early, sent, other))
    chip = index // 2

    def keep(block):
        inside = (block >= 0) & (block < count)
        return jnp.where(inside & (edges(block) == edges(block + 1)), 1.0, 0.0)

    keep_near = keep(2 * chip + (1 if step > 0 else 0))
    pair = joined(*[n + keep_near * f for n, f in zip(near, far)])
    arrived = [parted(chip_shift(pair, count // 2, step * (k + 1))) for k in range(CHIP_SPAN)]
    total = list(arrived[0])
    through = jnp.float32(1.0)
    for k in range(1, CHIP_SPAN):
        base = 2 * (chip - step * k)
        through = through * keep(base) * keep(base + 1)
        total = [t + through * a for t, a in zip(total, arrived[k])]
    first_kept = keep(2 * chip + (0 if step > 0 else 1))
    return [jnp.where(early, t, f + first_kept * t) for f, t in zip(far, total)]


def product(attended, full_out, parity, count):
    chip = lax.axis_index("ctx") // 2
    width = full_out.shape[1] // count
    picked = [
        lax.dynamic_slice_in_dim(full_out, (((r ^ chip) * 2) + parity) * width, width, 1)
        for r in range(count // 2)
    ]
    return lax.dot_general(
        attended,
        jnp.concatenate(picked, axis=1),
        (((0,), (0,)), ((), ())),
        preferred_element_type=f32,
    )


def leaving_part(attended, full_out, count):
    return product(attended, full_out, 1 - lax.axis_index("ctx") % 2, count).astype(bf16)


def reduce_halves(attended, full_out, came, count):
    chips = count // 2
    width = full_out.shape[1] // count
    rows = attended.shape[1]
    mine = product(attended, full_out, lax.axis_index("ctx") % 2, count) + came.astype(f32)
    bits = max(1, chips).bit_length() - 1
    half = rows // 2
    flows = []
    for flow, order in ((0, list(range(bits))), (1, list(range(bits))[::-1])):
        held = {
            r: mine[flow * half : (flow + 1) * half, r * width : (r + 1) * width]
            for r in range(chips)
        }
        for bit in order:
            moving = [r for r in held if (r >> bit) & 1]
            packed = jnp.concatenate([held[r].astype(bf16) for r in moving], axis=1)
            got = lax.ppermute(
                packed,
                "ctx",
                [(2 * c + k, 2 * (c ^ (1 << bit)) + k) for c in range(chips) for k in range(2)],
            )
            for place, r in enumerate(moving):
                target = r ^ (1 << bit)
                held[target] = held[target] + got[:, place * width : (place + 1) * width].astype(f32)
                del held[r]
        flows.append(held[0])
    return jnp.concatenate(flows, axis=0)


def on_device(query_key, values, out_grad, out_weight, doc_lengths):
    tokens = query_key.shape[0]
    head_count = out_weight.shape[0] // HEAD
    count = lax.axis_size("ctx")
    depth = lax.axis_size("head")
    level = lax.axis_index("head")
    shard = out_grad.shape[1]
    index = lax.axis_index("ctx")
    offset = index * tokens

    parts = [out_grad] + [
        lax.ppermute(out_grad, "head", [(i, i ^ d) for i in range(depth)]) for d in range(1, depth)
    ]
    weight_parts = [
        lax.dynamic_slice_in_dim(out_weight, (level ^ d) * shard, shard, 1) for d in range(depth)
    ]

    starts = jnp.cumsum(doc_lengths, dtype=jnp.int32) - doc_lengths

    def edges(block):
        return jnp.sum((starts <= block * tokens - 1).astype(jnp.int32)) - 1

    positions = offset + jnp.arange(tokens, dtype=jnp.int32)
    segment = segment_ids(doc_lengths, positions)
    open_before = edges(index)
    open_after = segment[tokens - 1]
    carried = (segment == open_before).astype(f32)[None, :, None]
    ending = (segment == open_after).astype(f32)[None, :, None]
    paired = query_key.reshape(tokens, head_count, 2, QK).transpose(1, 2, 0, 3)
    queries = paired[:, 0]
    keys_all = paired[:, 1]
    value_rows = values.reshape(tokens, head_count, HEAD).transpose(1, 0, 2)
    query_first, query_second = factors(queries)
    key_first, key_second = factors(keys_all)
    query_feat = (query_first * query_second * SCALE).astype(bf16)
    key_feat = (key_first * key_second * SCALE).astype(bf16)
    ending_feat = jnp.where(ending > 0.5, key_feat, jnp.zeros_like(key_feat))
    state_local = dot("htf,htd->hfd", ending_feat, value_rows)
    norm_local = jnp.sum(ending_feat.astype(f32), axis=1)
    state_in, norm_in = carried_in(joined(state_local, norm_local), edges, 1, count)
    state_b = state_in.astype(bf16)
    query_weighted = query_feat * jnp.asarray(WEIGHT, bf16)
    places = jnp.arange(tokens, dtype=jnp.int32)
    scores = dot("hid,hjd->hij", queries, keys_all) * 0.25
    visible = (places[None, :] <= places[:, None]) & (segment[:, None] == segment[None, :])
    weight = jnp.where(visible[None], 1.0 + scores + 0.5 * scores * scores, 0.0)
    weight_b = weight.astype(bf16)
    from_state = dot("hif,hfd->hid", query_weighted, state_b)
    numerator = dot("hij,hjd->hid", weight_b, value_rows) + carried * from_state
    denominator = (
        jnp.sum(weight, axis=2, keepdims=True)
        + carried
        * jnp.sum(query_weighted.astype(f32) * norm_in[:, None, :], axis=2, keepdims=True)
    )
    attended = numerator / denominator
    attended_all = (
        attended.astype(bf16).transpose(1, 0, 2).reshape(tokens, head_count * HEAD)
    )
    slots = []
    for place in range(depth):
        picked = parts[place]
        for d in range(1, depth):
            picked = jnp.where(level == d, parts[place ^ d], picked)
        slots.append(picked)
    full_out = jnp.concatenate(slots, axis=1)
    leaving = leaving_part(attended_all, full_out, count)
    leaving, parts = lax.optimization_barrier((leaving, parts))
    came = lax.ppermute(leaving, "ctx", [(c, c ^ 1) for c in range(count)])
    out_rows = sum(
        lax.dot_general(
            part, weight_part, (((1,), (1,)), ((), ())), preferred_element_type=f32
        )
        for part, weight_part in zip(parts, weight_parts)
    )

    grads_out = out_rows.reshape(tokens, head_count, HEAD).transpose(1, 0, 2)
    den_grad = -jnp.sum(grads_out * attended, axis=2, keepdims=True) / denominator
    num_grad = (grads_out / denominator).astype(bf16)
    near_feat = jnp.where(carried > 0.5, query_feat, jnp.zeros_like(query_feat))
    adj_local = dot("hif,hid->hfd", near_feat, num_grad)
    nadj_local = jnp.sum(near_feat.astype(f32) * den_grad, axis=1)
    adj_sent, full_out = lax.optimization_barrier((joined(adj_local, nadj_local), full_out))
    adj_in, nadj_in = carried_in(adj_sent, edges, -1, count)
    proj_grad = reduce_halves(attended_all, full_out, came, count)
    adjoint_b = adj_in.astype(bf16)

    mix_grad = dot("hid,hjd->hij", num_grad, value_rows) + den_grad
    score_grad = jnp.where(visible[None], mix_grad * (1.0 + scores), 0.0).astype(bf16)
    value_grad = dot("hij,hid->hjd", weight_b, num_grad)
    key_grad = 0.25 * dot("hij,hid->hjd", score_grad, queries)
    feat_grad = carried * (
        dot("hid,hfd->hif", num_grad, state_b) + den_grad * norm_in[:, None, :]
    )
    query_grad = 0.25 * dot("hij,hjd->hid", score_grad, keys_all) + feature_grad(
        feat_grad, query_first, query_second
    )
    value_grad = value_grad + ending * dot(
        "htf,hfd->htd", key_feat * jnp.asarray(WEIGHT, bf16), adjoint_b
    )
    key_feat_grad = ending * (
        dot("htd,hfd->htf", value_rows, adjoint_b) + nadj_in[:, None, :]
    )
    key_grad = key_grad + feature_grad(key_feat_grad, key_first, key_second)
    qk_grad = (
        jnp.stack([query_grad, key_grad], axis=2)
        .transpose(1, 0, 2, 3)
        .reshape(tokens, head_count * 2 * QK)
        .astype(bf16)
    )
    value_out = (
        value_grad.transpose(1, 0, 2).reshape(tokens, head_count * HEAD).astype(bf16)
    )
    return (qk_grad, value_out, proj_grad)


def solution(mesh):
    placed = (P("ctx", "head"), P("ctx", "head"), P("ctx", "head"), P("head", None), P())
    return jax.shard_map(
        on_device,
        mesh=mesh,
        in_specs=placed,
        out_specs=(P("ctx", "head"), P("ctx", "head"), P("head", "ctx")),
        check_vma=False,
    )
```

```python
import math

import jax
import jax.numpy as jnp
import numpy as np
from jax import lax
from jax.sharding import PartitionSpec as P

HEAD = 128
QK = 16
CHIP_SPAN = 2

quad_scale = 0.25 / math.sqrt(2.0)

bf16 = jnp.bfloat16
f32 = jnp.float32

PAIRS = [(a, b) for a in range(QK) for b in range(a, QK)]
KEPT = 1 + QK + len(PAIRS)
FEAT = 160


def tables():
    left = np.zeros((QK, FEAT), np.float32)
    right = np.zeros((QK, FEAT), np.float32)
    left_add = np.zeros((FEAT,), np.float32)
    right_add = np.zeros((FEAT,), np.float32)
    scale = np.zeros((FEAT,), np.float32)
    weight = np.ones((FEAT,), np.float32)
    left_add[0] = right_add[0] = scale[0] = 1.0
    for a in range(QK):
        left[a, 1 + a] = 1.0
        right_add[1 + a] = 1.0
        scale[1 + a] = 0.5
    for place, (a, b) in enumerate(PAIRS):
        left[a, 1 + QK + place] = 1.0
        right[b, 1 + QK + place] = 1.0
        scale[1 + QK + place] = quad_scale
        weight[1 + QK + place] = 1.0 if a == b else 2.0
    return left, right, left_add, right_add, scale, weight


LEFT, RIGHT, LEFT_ADD, RIGHT_ADD, SCALE, WEIGHT = tables()


def dot(spec, a, b):
    return jnp.einsum(spec, a, b, preferred_element_type=f32)


def factors(points):
    first = dot("htd,df->htf", points, jnp.asarray(LEFT, bf16)) + LEFT_ADD
    second = dot("htd,df->htf", points, jnp.asarray(RIGHT, bf16)) + RIGHT_ADD
    return first, second


def feature_grad(grad_feat, first, second):
    scaled = grad_feat * (SCALE * WEIGHT)
    return dot("htf,df->htd", (scaled * second).astype(bf16), jnp.asarray(LEFT, bf16)) + dot(
        "htf,df->htd", (scaled * first).astype(bf16), jnp.asarray(RIGHT, bf16)
    )


def segment_ids(doc_lengths, positions):
    starts = jnp.cumsum(doc_lengths, dtype=jnp.int32) - doc_lengths
    return jnp.sum((starts[None, :] <= positions[:, None]).astype(jnp.int32), axis=1) - 1


def chip_shift(part, chips, steps):
    moves = [
        (2 * c + core, 2 * (c + steps) + core)
        for c in range(chips)
        for core in range(2)
        if 0 <= c + steps < chips
    ]
    return lax.ppermute(part, "ctx", moves)


def joined(state, norm):
    half = norm.shape[1] // 2
    high = norm.astype(bf16).astype(f32)
    low = norm - high
    rows = jnp.stack([high[:, :half], high[:, half:], low[:, :half], low[:, half:]], axis=1)
    rows = jnp.pad(rows, ((0, 0), (KEPT, FEAT - KEPT - 4), (0, HEAD - half)))
    return (state + rows).astype(bf16)


def parted(packed):
    half = FEAT // 2
    rows = packed[:, KEPT : KEPT + 4, :half].astype(f32)
    norm = jnp.concatenate([rows[:, 0] + rows[:, 2], rows[:, 1] + rows[:, 3]], axis=1)
    inside = (jnp.arange(FEAT) < KEPT)[None, :, None]
    return jnp.where(inside, packed.astype(f32), 0.0), norm


def carried_in(sent, edges, step, count, at_pair, at_arrived):
    index = lax.axis_index("ctx")
    core = index % 2
    other = lax.ppermute(sent, "ctx", [(c, c ^ 1) for c in range(count)])
    early = core == (0 if step > 0 else 1)
    near = parted(jnp.where(early, other, sent))
    far = parted(jnp.where(early, sent, other))
    chip = index // 2

    def keep(block):
        inside = (block >= 0) & (block < count)
        return jnp.where(inside & (edges(block) == edges(block + 1)), 1.0, 0.0)

    keep_near = keep(2 * chip + (1 if step > 0 else 0))
    pair = at_pair(joined(*[n + keep_near * f for n, f in zip(near, far)]))
    arrived = [chip_shift(pair, count // 2, step * (k + 1)) for k in range(CHIP_SPAN)]
    arrived = [parted(one) for one in at_arrived(arrived)]
    total = list(arrived[0])
    through = jnp.float32(1.0)
    for k in range(1, CHIP_SPAN):
        base = 2 * (chip - step * k)
        through = through * keep(base) * keep(base + 1)
        total = [t + through * a for t, a in zip(total, arrived[k])]
    first_kept = keep(2 * chip + (0 if step > 0 else 1))
    return [jnp.where(early, t, f + first_kept * t) for f, t in zip(far, total)]


def product(attended, full_out, parity, count):
    chip = lax.axis_index("ctx") // 2
    width = full_out.shape[1] // count
    picked = [
        lax.dynamic_slice_in_dim(full_out, (((r ^ chip) * 2) + parity) * width, width, 1)
        for r in range(count // 2)
    ]
    return lax.dot_general(
        attended,
        jnp.concatenate(picked, axis=1),
        (((0,), (0,)), ((), ())),
        preferred_element_type=f32,
    )


def leaving_part(attended, full_out, count):
    return product(attended, full_out, 1 - lax.axis_index("ctx") % 2, count).astype(bf16)


def reduce_halves(mine, count):
    chips = count // 2
    width = mine.shape[1] // chips
    rows = mine.shape[0]
    bits = max(1, chips).bit_length() - 1
    half = rows // 2
    flows = []
    for flow, order in ((0, list(range(bits))), (1, list(range(bits))[::-1])):
        held = {
            r: mine[flow * half : (flow + 1) * half, r * width : (r + 1) * width]
            for r in range(chips)
        }
        for bit in order:
            moving = [r for r in held if (r >> bit) & 1]
            packed = jnp.concatenate([held[r].astype(bf16) for r in moving], axis=1)
            got = lax.ppermute(
                packed,
                "ctx",
                [(2 * c + k, 2 * (c ^ (1 << bit)) + k) for c in range(chips) for k in range(2)],
            )
            for place, r in enumerate(moving):
                target = r ^ (1 << bit)
                held[target] = held[target] + got[:, place * width : (place + 1) * width].astype(f32)
                del held[r]
        flows.append(held[0])
    return jnp.concatenate(flows, axis=0)


def on_device(query_key, values, out_grad, out_weight, doc_lengths):
    tokens = query_key.shape[0]
    head_count = out_weight.shape[0] // HEAD
    count = lax.axis_size("ctx")
    depth = lax.axis_size("head")
    level = lax.axis_index("head")
    shard = out_grad.shape[1]
    index = lax.axis_index("ctx")
    offset = index * tokens

    up, down = [out_grad], [out_grad]

    def advance(passed):
        k = len(up)
        if k >= depth:
            return passed
        if k > 1:
            up[-1], down[-1], passed = lax.optimization_barrier((up[-1], down[-1], passed))
        up.append(lax.ppermute(up[-1], "head", [(i, i + 1) for i in range(k - 1, depth - 1)]))
        down.append(lax.ppermute(down[-1], "head", [(i, i - 1) for i in range(1, depth - k + 1)]))
        return passed

    advance(None)

    starts = jnp.cumsum(doc_lengths, dtype=jnp.int32) - doc_lengths

    def edges(block):
        return jnp.sum((starts <= block * tokens - 1).astype(jnp.int32)) - 1

    positions = offset + jnp.arange(tokens, dtype=jnp.int32)
    segment = segment_ids(doc_lengths, positions)
    open_before = edges(index)
    open_after = segment[tokens - 1]
    carried = (segment == open_before).astype(f32)[None, :, None]
    ending = (segment == open_after).astype(f32)[None, :, None]
    paired = query_key.reshape(tokens, head_count, 2, QK).transpose(1, 2, 0, 3)
    queries = paired[:, 0]
    keys_all = paired[:, 1]
    value_rows = values.reshape(tokens, head_count, HEAD).transpose(1, 0, 2)
    query_first, query_second = factors(queries)
    key_first, key_second = factors(keys_all)
    query_feat = (query_first * query_second * SCALE).astype(bf16)
    key_feat = (key_first * key_second * SCALE).astype(bf16)
    ending_feat = jnp.where(ending > 0.5, key_feat, jnp.zeros_like(key_feat))
    state_local = dot("htf,htd->hfd", ending_feat, value_rows)
    norm_local = jnp.sum(ending_feat.astype(f32), axis=1)
    query_weighted = query_feat * jnp.asarray(WEIGHT, bf16)
    places = jnp.arange(tokens, dtype=jnp.int32)
    scores = dot("hid,hjd->hij", queries, keys_all) * 0.25
    visible = (places[None, :] <= places[:, None]) & (segment[:, None] == segment[None, :])
    weight = jnp.where(visible[None], 1.0 + scores + 0.5 * scores * scores, 0.0)
    weight_b = weight.astype(bf16)
    local_sum = dot("hij,hjd->hid", weight_b, value_rows)

    def after_shift(arrived):
        nonlocal local_sum
        arrived, local_sum = advance((arrived, local_sum))
        while len(up) < depth:
            local_sum = advance(local_sum)
        return arrived

    state_in, norm_in = carried_in(
        joined(state_local, norm_local), edges, 1, count, advance, after_shift
    )
    state_b = state_in.astype(bf16)
    from_state = dot("hif,hfd->hid", query_weighted, state_b)
    numerator = local_sum + carried * from_state
    denominator = (
        jnp.sum(weight, axis=2, keepdims=True)
        + carried
        * jnp.sum(query_weighted.astype(f32) * norm_in[:, None, :], axis=2, keepdims=True)
    )
    attended = numerator / denominator
    attended_all = (
        attended.astype(bf16).transpose(1, 0, 2).reshape(tokens, head_count * HEAD)
    )
    slots = []
    for place in range(depth):
        picked = out_grad
        for at in range(depth):
            if at != place:
                picked = jnp.where(
                    level == at, up[at - place] if at > place else down[place - at], picked
                )
        slots.append(picked)
    full_out = jnp.concatenate(slots, axis=1)
    leaving = leaving_part(attended_all, full_out, count)

    pieces = [(out_grad, level)]
    for k in range(1, depth):
        if 2 * k >= depth:
            below = level >= k
            pieces.append(
                (jnp.where(below, up[k], down[k]), jnp.where(below, level - k, level + k))
            )
        else:
            pieces += [(up[k], level - k), (down[k], level + k)]
    out_rows = 0.0
    for n, (part, owner) in enumerate(pieces):
        if n == len(pieces) - 1:
            leaving, part = lax.optimization_barrier((leaving, part))
        weight_part = lax.dynamic_slice_in_dim(
            out_weight, jnp.clip(owner, 0, depth - 1) * shard, shard, 1
        )
        out_rows = out_rows + lax.dot_general(
            part, weight_part, (((1,), (1,)), ((), ())), preferred_element_type=f32
        )
    came = lax.ppermute(leaving, "ctx", [(c, c ^ 1) for c in range(count)])

    grads_out = out_rows.reshape(tokens, head_count, HEAD).transpose(1, 0, 2)
    den_grad = -jnp.sum(grads_out * attended, axis=2, keepdims=True) / denominator
    num_grad = (grads_out / denominator).astype(bf16)
    near_feat = jnp.where(carried > 0.5, query_feat, jnp.zeros_like(query_feat))
    adj_local = dot("hif,hid->hfd", near_feat, num_grad)
    nadj_local = jnp.sum(near_feat.astype(f32) * den_grad, axis=1)
    adj_sent, full_out = lax.optimization_barrier((joined(adj_local, nadj_local), full_out))
    mine = product(attended_all, full_out, index % 2, count) + came.astype(f32)

    def with_product(arrived):
        nonlocal mine
        arrived, mine = lax.optimization_barrier((arrived, mine))
        return arrived

    adj_in, nadj_in = carried_in(adj_sent, edges, -1, count, lambda pair: pair, with_product)
    proj_grad = reduce_halves(mine, count)
    adjoint_b = adj_in.astype(bf16)

    mix_grad = dot("hid,hjd->hij", num_grad, value_rows) + den_grad
    score_grad = jnp.where(visible[None], mix_grad * (1.0 + scores), 0.0).astype(bf16)
    value_grad = dot("hij,hid->hjd", weight_b, num_grad)
    key_grad = 0.25 * dot("hij,hid->hjd", score_grad, queries)
    feat_grad = carried * (
        dot("hid,hfd->hif", num_grad, state_b) + den_grad * norm_in[:, None, :]
    )
    query_grad = 0.25 * dot("hij,hjd->hid", score_grad, keys_all) + feature_grad(
        feat_grad, query_first, query_second
    )
    value_grad = value_grad + ending * dot(
        "htf,hfd->htd", key_feat * jnp.asarray(WEIGHT, bf16), adjoint_b
    )
    key_feat_grad = ending * (
        dot("htd,hfd->htf", value_rows, adjoint_b) + nadj_in[:, None, :]
    )
    key_grad = key_grad + feature_grad(key_feat_grad, key_first, key_second)
    qk_grad = (
        jnp.stack([query_grad, key_grad], axis=2)
        .transpose(1, 0, 2, 3)
        .reshape(tokens, head_count * 2 * QK)
        .astype(bf16)
    )
    value_out = (
        value_grad.transpose(1, 0, 2).reshape(tokens, head_count * HEAD).astype(bf16)
    )
    return (qk_grad, value_out, proj_grad)


def solution(mesh):
    placed = (P("ctx", "head"), P("ctx", "head"), P("ctx", "head"), P("head", None), P())
    return jax.shard_map(
        on_device,
        mesh=mesh,
        in_specs=placed,
        out_specs=(P("ctx", "head"), P("ctx", "head"), P("head", "ctx")),
        check_vma=False,
    )
```
